128 devices in a mesh: wide: 16 (over x, z_lo, core), narrow: 8 (over z_hi, y).
Axes of the slice: x: 4, y: 4, z: 4 (z_hi: 2, z_lo: 2; z = z_hi * 2 + z_lo), core: 2. Of those that a mesh axis runs over, the one named last changes fastest.
Arguments:
- amplitudes: float32 [2, 16, 8, 16, 256, 256], P(None, 'wide', 'narrow'), may hold values from -6 to 6
- low_gate: float32 [2, 256, 256], replicated, may hold values from -0.25 to 0.25
- mid_gate: float32 [2, 256, 256], replicated, may hold values from -0.25 to 0.25
- pair_gates: float32 [3, 2, 4, 4], replicated, may hold values from -2 to 2
Outputs:
- remapped: float32 [2, 16, 8, 16, 256, 256], P(None, 'wide', 'narrow')
The draws below stay inside these ranges and needn't reach their ends.
All inputs are finite; a program needn't handle non-finite values.
Results may differ from the reference program's by a relative error of at most 0.00007.
Values sent between devices are 32-bit elements; how exact they have to be, the bound alone decides.
No kernel may reach another device: no remote copies, remote signals or barrier semaphores. Data moves between devices by JAX's collectives and lax.ppermute only.
A program may use at most 128 MiB of HBM per device.

```python
import jax
import jax.numpy as jnp
from jax import lax

GATE = 256
HI = 16
N_WIDE = 16
N_NARROW = 8


def level_of(own_key, extent, cuts, low, top_value):
    gain, own = 1.0, jax.random.fold_in(own_key, 6)
    for dim, shards_of in cuts:
        draws = jnp.exp(jax.random.uniform(jax.random.fold_in(own, dim), (shards_of,), jnp.float32, low / len(cuts), top_value / len(cuts)))
        gain = gain * jnp.repeat(draws, extent[dim] // shards_of).reshape([-1 if axis == dim else 1 for axis in range(len(extent))])
    return gain


def centred(stream_key, extent, scale, most, cuts=(), kind=jnp.bfloat16):
    factor_of = level_of(stream_key, extent, cuts, -0.22, 0.18) if cuts else 1.0
    array = jax.random.normal(stream_key, extent, jnp.float32) * scale * factor_of
    return jnp.minimum(jnp.maximum(array, -most), most).astype(kind)


def setup_inputs(seed: int = 0) -> dict:
    key_list = jax.random.split(jax.random.key(seed), 5)
    amplitudes = centred(key_list[0], (2, N_WIDE, N_NARROW, HI, GATE, GATE), 1.0, 6.0, ((1, 16), (2, 8)), jnp.float32)
    low_gate = centred(key_list[1], (2, GATE, GATE), (2 * GATE) ** -0.5, 0.25, (), jnp.float32)
    mid_gate = centred(key_list[2], (2, GATE, GATE), (2 * GATE) ** -0.5, 0.25, (), jnp.float32)
    pair_gates = centred(key_list[3], (3, 2, 4, 4), 8 ** -0.5, 2.0, (), jnp.float32)
    return dict(amplitudes=amplitudes, low_gate=low_gate, mid_gate=mid_gate, pair_gates=pair_gates)


highest = lax.Precision.HIGHEST


def merged_block(block, low_gate, mid_gate):
    real_part, imag_part = block[0], block[1]
    low_real, low_imag = low_gate[0], low_gate[1]
    first_real = jnp.einsum('nhml,il->nhmi', real_part, low_real, precision=highest) - jnp.einsum('nhml,il->nhmi', imag_part, low_imag, precision=highest)
    first_imag = jnp.einsum('nhml,il->nhmi', real_part, low_imag, precision=highest) + jnp.einsum('nhml,il->nhmi', imag_part, low_real, precision=highest)
    mid_real, mid_imag = mid_gate[0], mid_gate[1]
    second_real = jnp.einsum('nhml,im->nhil', first_real, mid_real, precision=highest) - jnp.einsum('nhml,im->nhil', first_imag, mid_imag, precision=highest)
    second_imag = jnp.einsum('nhml,im->nhil', first_real, mid_imag, precision=highest) + jnp.einsum('nhml,im->nhil', first_imag, mid_real, precision=highest)
    return jnp.stack([second_real, second_imag])


def bit_gate(state, gate, first_axis, first_bit, second_bit):
    shape = state.shape
    second_axis = 3
    new_shape = list(shape[:first_axis]) + [shape[first_axis] >> (first_bit + 1), 2, 1 << first_bit] + list(shape[first_axis + 1:second_axis]) + [shape[second_axis] >> (second_bit + 1), 2, 1 << second_bit] + list(shape[second_axis + 1:])
    first_pos = first_axis + 1
    second_pos = second_axis + 3
    split = jnp.moveaxis(state.reshape(new_shape), (first_pos, second_pos), (1, 2))
    gate_four = gate.reshape(2, 2, 2, 2, 2)
    real_new = jnp.einsum('pqab,ab...->pq...', gate_four[0], split[0], precision=highest) - jnp.einsum('pqab,ab...->pq...', gate_four[1], split[1], precision=highest)
    imag_new = jnp.einsum('pqab,ab...->pq...', gate_four[0], split[1], precision=highest) + jnp.einsum('pqab,ab...->pq...', gate_four[1], split[0], precision=highest)
    joined = jnp.stack([real_new, imag_new])
    return jnp.moveaxis(joined, (1, 2), (first_pos, second_pos)).reshape(shape)


def remap_state(state):
    shape = state.shape
    wide_count = shape[1]
    width = shape[4]
    parts = state.reshape(2, wide_count, shape[2], shape[3], wide_count, width // wide_count, shape[5])
    moved = jnp.transpose(parts, (0, 4, 2, 3, 1, 5, 6))
    return moved.reshape(shape)


def reference(amplitudes, low_gate, mid_gate, pair_gates):
    moved = jnp.moveaxis(amplitudes, 1, 0)

    def one_block(block_now):
        return merged_block(block_now, low_gate, mid_gate)

    mixed = lax.map(one_block, moved)
    state = jnp.moveaxis(mixed, 0, 1)
    state = bit_gate(state, pair_gates[0], 1, 0, 0)
    state = bit_gate(state, pair_gates[1], 1, 2, 1)
    state = bit_gate(state, pair_gates[2], 2, 1, 0)
    return remap_state(state)
```

```python
import functools

import jax
import jax.numpy as jnp
from jax import lax
from jax.experimental import pallas as pl
from jax.experimental.pallas import tpu as pltpu
from jax.sharding import PartitionSpec as P

f32, bf16 = jnp.float32, jnp.bfloat16
G = 256
ROWS = 16
CHUNK = 4


def hbm(x):
    return pltpu.with_memory_space_constraint(x, pltpu.HBM)


def split(x):
    high = x.astype(bf16)
    return high, (x - high.astype(f32)).astype(bf16)


def prep_kernel(g_ref, high_ref, low_ref):
    real, imag = g_ref[0], g_ref[1]
    for (row, col), part in (((0, 0), real), ((0, 1), -imag), ((1, 0), imag), ((1, 1), real)):
        high, low = split(part)
        high_ref[row * G : (row + 1) * G, col * G : (col + 1) * G] = high
        low_ref[row * G : (row + 1) * G, col * G : (col + 1) * G] = low


def prepare(gate):
    return pl.pallas_call(
        prep_kernel,
        out_shape=[jax.ShapeDtypeStruct((2 * G, 2 * G), bf16)] * 2,
        cost_estimate=pl.CostEstimate(flops=1, bytes_accessed=1, transcendentals=0),
        compiler_params=pltpu.CompilerParams(vmem_limit_bytes=60 << 20),
        name="prep",
    )(gate)


def merged_kernel(start_ref, x_ref, low_high, low_low, mid_high, mid_low, o_ref):
    x = jnp.concatenate([x_ref[0, 0], x_ref[1, 0]], axis=1)
    x_high, x_low = split(x)
    transposed = (((1,), (1,)), ((), ()))

    def right(a, b):
        return lax.dot_general(a, b, transposed, preferred_element_type=f32)

    def left(a, b):
        return jnp.dot(a, b, preferred_element_type=f32)

    t = right(x_high, low_high[...]) + right(x_high, low_low[...]) + right(x_low, low_high[...])
    t = jnp.concatenate([t[:, :G], t[:, G:]], axis=0)
    t_high, t_low = split(t)
    s = left(mid_high[...], t_high) + left(mid_high[...], t_low) + left(mid_low[...], t_high)
    o_ref[:, 0, 0] = s[:G].reshape(G // ROWS, ROWS, G)
    o_ref[:, 1, 0] = s[G:].reshape(G // ROWS, ROWS, G)


def merged(x, start, gates, count, weight=1):
    whole = pl.BlockSpec((2 * G, 2 * G), lambda i, s: (0, 0))
    return pl.pallas_call(
        merged_kernel,
        out_shape=jax.ShapeDtypeStruct((G // ROWS, 2, count, ROWS, G), f32),
        grid_spec=pltpu.PrefetchScalarGridSpec(
            num_scalar_prefetch=1,
            grid=(count,),
            in_specs=[pl.BlockSpec((2, 1, G, G), lambda i, s: (0, s[0] + i, 0, 0))] + [whole] * 4,
            out_specs=pl.BlockSpec((G // ROWS, 2, 1, ROWS, G), lambda i, s: (0, 0, i, 0, 0)),
        ),
        cost_estimate=pl.CostEstimate(
            flops=weight, bytes_accessed=1, transcendentals=0
        ),
        compiler_params=pltpu.CompilerParams(vmem_limit_bytes=60 << 20),
        name="merged",
    )(start, hbm(x), *gates)


def combine(coef, amps):
    outs = []
    for row in range(4):
        real = imag = None
        for col in range(4):
            cr, ci = coef(row, col)
            ar, ai = amps[col]
            real = cr * ar if real is None else real + cr * ar
            real = real - ci * ai
            imag = cr * ai if imag is None else imag + cr * ai
            imag = imag + ci * ar
        outs.append((real, imag))
    return outs


def pair_kernel(bit_ref, gate_ref, own_ref, far_ref, *refs):
    out_ref, back_ref, scratch = refs[-3:]
    own = bit_ref[0]
    sources = (own_ref, far_ref)
    targets = (out_ref, back_ref)

    def plain(k):
        def coef(row, col):
            return gate_ref[((2 * k) * 4 + row) * 4 + col], gate_ref[((2 * k + 1) * 4 + row) * 4 + col]

        return coef

    narrow_bit = (own, 1 - own)

    def narrow(row, col):
        r = 2 * narrow_bit[row >> 1] + (row & 1)
        c = 2 * narrow_bit[col >> 1] + (col & 1)
        at = 4 * r + c
        return gate_ref[64 + at], gate_ref[80 + at]

    def tile(step, carry):
        lanes = pl.ds(pl.multiple_of(step * 128, 128), 128)
        for n in range(2):
            for w0 in range(2):
                for h0 in range(2):
                    where = [(w2, w0, 2 * h1 + h0) for w2 in range(2) for h1 in range(2)]
                    amps = [tuple(sources[n][a, b, c, h, :, lanes] for c in range(2)) for a, b, h in where]
                    for (a, b, h), value in zip(where, combine(plain(1), amps)):
                        for c in range(2):
                            scratch[n, a, b, c, h] = value[c]
        for w2 in range(2):
            for h1 in range(2):
                state = {}
                for n in range(2):
                    where = [(w0, h0) for w0 in range(2) for h0 in range(2)]
                    amps = [tuple(scratch[n, w2, w0, c, 2 * h1 + h0] for c in range(2)) for w0, h0 in where]
                    for (w0, h0), value in zip(where, combine(plain(0), amps)):
                        state[n, w0, h0] = value
                for w0 in range(2):
                    where = [(n, h0) for n in range(2) for h0 in range(2)]
                    amps = [state[n, w0, h0] for n, h0 in where]
                    for (n, h0), value in zip(where, combine(narrow, amps)):
                        for c in range(2):
                            targets[n][c, 2 * h1 + h0, w2, w0, :, lanes] = value[c]
        return carry

    lax.fori_loop(0, 2, tile, 0)


def pair(bit, gates, own, far, chunk, base, count, held):
    shape = (2, 2, 2, 2, 2, CHUNK, ROWS, G)
    source = pl.BlockSpec((None, 2, None, 2, 2, CHUNK, 8, G), lambda i, j, r, s, g: (i, 0, j, 0, 0, 0, base + r, 0))
    full = (2, 4, CHUNK, 2, 2, 2, 2, ROWS, G)
    back = (2, CHUNK, 2, 2, 2, 2, 8 * count, G)
    out_spec = pl.BlockSpec(
        (2, None, CHUNK, None, 2, None, 2, 8, G),
        lambda i, j, r, s, g: (0, 2 * s[0] + chunk, 0, i, 0, j, 0, base + r, 0),
    )
    back_spec = pl.BlockSpec((2, CHUNK, None, 2, None, 2, 8, G), lambda i, j, r, s, g: (0, 0, i, 0, j, 0, r, 0))
    extra = [] if held is None else [held.reshape(full)]
    held, back = pl.pallas_call(
        pair_kernel,
        out_shape=[jax.ShapeDtypeStruct(full, f32), jax.ShapeDtypeStruct(back, f32)],
        grid_spec=pltpu.PrefetchScalarGridSpec(
            num_scalar_prefetch=2,
            grid=(2, 2, count),
            in_specs=[source, source] + [pl.BlockSpec(memory_space=pl.ANY)] * len(extra),
            out_specs=[out_spec, back_spec],
            scratch_shapes=[pltpu.VMEM((2, 2, 2, 2, CHUNK, 8, 128), f32)],
        ),
        input_output_aliases={4: 0} if extra else {},
        cost_estimate=pl.CostEstimate(flops=1, bytes_accessed=1, transcendentals=0),
        compiler_params=pltpu.CompilerParams(vmem_limit_bytes=16 << 20),
        name="pair",
    )(bit, gates, own.reshape(shape), far.reshape(shape), *extra)
    return held, back.reshape(2, CHUNK, 16, 8 * count, G)


def place_kernel(bit_ref, piece_ref, held_ref, out_ref):
    out_ref[...] = piece_ref[...]


def place(bit, piece, chunk, base, count, held, weight=1):
    full = (2, 4, CHUNK, 16, ROWS, G)
    return pl.pallas_call(
        place_kernel,
        out_shape=jax.ShapeDtypeStruct(full, f32),
        grid_spec=pltpu.PrefetchScalarGridSpec(
            num_scalar_prefetch=1,
            grid=(CHUNK,),
            in_specs=[
                pl.BlockSpec((2, 1, 16, 8 * count, G), lambda h, s: (0, h, 0, 0, 0)),
                pl.BlockSpec(memory_space=pl.ANY),
            ],
            out_specs=pl.BlockSpec(
                (2, None, 1, 16, 8 * count, G), lambda h, s: (0, 2 * (1 - s[0]) + chunk, h, 0, base, 0)
            ),
        ),
        input_output_aliases={2: 0},
        cost_estimate=pl.CostEstimate(flops=weight, bytes_accessed=1, transcendentals=0),
        compiler_params=pltpu.CompilerParams(vmem_limit_bytes=16 << 20),
        name="place",
    )(bit, piece, held.reshape(full))


def body(amplitudes, low_gate, mid_gate, pair_gates):
    x = amplitudes.reshape(2, 16, G, G)
    bit = lax.axis_index("narrow") >> 1 & 1
    bits = bit.reshape(1).astype(jnp.int32)
    partners = [(i, i ^ 2) for i in range(lax.axis_size("narrow"))]

    def swapped(value):
        return lax.ppermute(value, "narrow", partners)

    def remap(value):
        return lax.all_to_all(value, "wide", split_axis=0, concat_axis=0, tiled=True)

    barrier = lax.optimization_barrier

    def piece(bit, k):
        return lax.dynamic_slice_in_dim(x, 8 * (1 - bit) + CHUNK * k, CHUNK, 1)

    bits, low_gate, sent = barrier((bits, low_gate, piece(bit, 0)))
    arrived = [swapped(sent), swapped(piece(bits[0], 1))]
    gates = (*prepare(low_gate), *prepare(mid_gate))
    flat = pair_gates.reshape(96)
    zero = jnp.zeros((1,), jnp.int32)

    own0 = remap(merged(x, 8 * bits, gates, CHUNK))
    first = merged(arrived[0], zero, gates, CHUNK)
    bits1, first = barrier((bits, first))
    own1 = remap(merged(x, 8 * bits1 + CHUNK, gates, CHUNK))
    far0 = remap(first)
    pieces = {}
    held, pieces[0, 0] = pair(bits, flat, own0, far0, 0, 0, 2, None)
    last, pieces[0, 0] = barrier((arrived[1], pieces[0, 0]))
    far1 = remap(merged(last, zero, gates, CHUNK, 20000000000))
    for half in range(2):
        held, pieces[1, half] = pair(bits, flat, own1, far1, 1, half, 1, held)
    backs = {key: swapped(piece) for key, piece in pieces.items()}
    held = place(bits, backs[0, 0], 0, 0, 2, held, 20000000000)
    for half in range(2):
        held = place(bits, backs[1, half], 1, half, 1, held, 1000000000)
    return held.reshape(amplitudes.shape)


def solution(mesh):
    in_specs = (P(None, "wide", "narrow", None, None, None), P(), P(), P())
    out_specs = P(None, "wide", "narrow", None, None, None)
    return jax.shard_map(body, mesh=mesh, in_specs=in_specs, out_specs=out_specs, check_vma=False)
```

```python
import jax
import jax.numpy as jnp
from jax import lax
from jax.experimental import pallas as pl
from jax.experimental.pallas import tpu as pltpu
from jax.sharding import PartitionSpec as P

f32, bf16 = jnp.float32, jnp.bfloat16
G = 256
ROWS = 16
CHUNK = 4
PAIR = 2


def cost(weight):
    return pl.CostEstimate(flops=weight, bytes_accessed=1, transcendentals=0)


def params(mib):
    return pltpu.CompilerParams(vmem_limit_bytes=mib << 20)


def hbm(x):
    return pltpu.with_memory_space_constraint(x, pltpu.HBM)


def split(x):
    high = x.astype(bf16)
    return high, (x - high.astype(f32)).astype(bf16)


def prep_kernel(low_ref, mid_ref, o_ref):
    for at, ref in enumerate((low_ref, mid_ref)):
        real, imag = ref[0], ref[1]
        for j, part in enumerate((real, imag - real, real + imag)):
            o_ref[at, j, 0], o_ref[at, j, 1] = split(part)


def prepare(low_gate, mid_gate):
    return pl.pallas_call(
        prep_kernel,
        out_shape=jax.ShapeDtypeStruct((2, 3, 2, G, G), bf16),
        cost_estimate=cost(1),
        compiler_params=params(60),
        name="prep",
    )(low_gate, mid_gate)


def merged_kernel(x_ref, g_ref, refs):

    def right(value, j):
        high, low = split(value)
        out = None
        for a, b in ((high, 0), (high, 1), (low, 0)):
            term = lax.dot_general(a, g_ref[0, j, b], (((1,), (1,)), ((), ())), preferred_element_type=f32)
            out = term if out is None else out + term
        return out

    def left(value, j):
        high, low = split(value)
        out = None
        for a, b in ((0, high), (0, low), (1, high)):
            term = jnp.dot(g_ref[1, j, a], b, preferred_element_type=f32)
            out = term if out is None else out + term
        return out

    def both(apply, real, imag):
        shared = apply(real + imag, 0)
        cross = apply(real, 1)
        return shared - apply(imag, 2), shared + cross

    firsts = [both(right, x_ref[0, i], x_ref[1, i]) for i in range(PAIR)]
    for i, first in enumerate(firsts):
        for c, value in enumerate(both(left, *first)):
            value = value.reshape(G // ROWS, ROWS, G)
            for at, o_ref in enumerate(refs):
                rows = ROWS // len(refs)
                o_ref[:, c, i] = value[:, at * rows : (at + 1) * rows]


def merged(x, start, gates, parts=1, part=0, held=(), weight=1):
    steps = CHUNK // PAIR
    rows = ROWS // parts
    out = jax.ShapeDtypeStruct((G // ROWS, 2, parts * CHUNK, rows, G), f32)
    spec = pl.BlockSpec((G // ROWS, 2, PAIR, rows, G), lambda i, s: (0, 0, part * steps + i, 0, 0))

    def kernel(start_ref, x_ref, g_ref, *refs):
        merged_kernel(x_ref, g_ref, refs[len(held) :])

    return pl.pallas_call(
        kernel,
        out_shape=[out] * parts,
        grid_spec=pltpu.PrefetchScalarGridSpec(
            num_scalar_prefetch=1,
            grid=(steps,),
            in_specs=[
                pl.BlockSpec((2, PAIR, G, G), lambda i, s: (0, s[0] * steps + i, 0, 0)),
                pl.BlockSpec((2, 3, 2, G, G), lambda i, s: (0, 0, 0, 0, 0)),
            ]
            + [pl.BlockSpec(memory_space=pl.ANY)] * len(held),
            out_specs=[spec] * parts,
        ),
        input_output_aliases={3 + j: j for j in range(len(held))},
        cost_estimate=cost(weight),
        compiler_params=params(60),
        name="merged",
    )(start, hbm(x), gates, *held)


def combine(coef, amps, rows=4):
    outs = []
    for row in range(rows):
        real = imag = None
        for col, (ar, ai) in enumerate(amps):
            cr, ci = coef(row, col)
            real = cr * ar - ci * ai if real is None else real + (cr * ar - ci * ai)
            imag = cr * ai + ci * ar if imag is None else imag + (cr * ai + ci * ar)
        outs.append((real, imag))
    return outs


def plain(gate_ref, k):
    def coef(row, col):
        return gate_ref[32 * k + 4 * row + col], gate_ref[32 * k + 16 + 4 * row + col]

    return coef


def narrow_coef(gate_ref, own):
    bit = (own, 1 - own)

    def coef(row, col):
        at = 64 + 4 * (2 * bit[row >> 1] + (row & 1)) + 2 * bit[col >> 1] + (col & 1)
        return gate_ref[at], gate_ref[at + 16]

    return coef


def wide_high(gate_ref, ref, out):
    for w0 in range(2):
        for h0 in range(2):
            where = [(w2, w0, 2 * h1 + h0) for w2 in range(2) for h1 in range(2)]
            amps = [(ref[a, b, 0, h], ref[a, b, 1, h]) for a, b, h in where]
            for (a, b, h), (real, imag) in zip(where, combine(plain(gate_ref, 1), amps)):
                out[a, b, 0, h], out[a, b, 1, h] = real, imag


def wide_low(gate_ref, ref, w2, h1):
    where = [(w0, h0) for w0 in range(2) for h0 in range(2)]
    amps = [(ref[w2, w0, 0, 2 * h1 + h0], ref[w2, w0, 1, 2 * h1 + h0]) for w0, h0 in where]
    return dict(zip(where, combine(plain(gate_ref, 0), amps)))


def local_kernel(gate_ref, x_ref, o_ref, scratch):
    wide_high(gate_ref, x_ref, scratch)
    for w2 in range(2):
        for h1 in range(2):
            for (w0, h0), (real, imag) in wide_low(gate_ref, scratch, w2, h1).items():
                o_ref[0, 2 * h1 + h0, w2, w0] = real
                o_ref[1, 2 * h1 + h0, w2, w0] = imag


def local(gates, x):
    return pl.pallas_call(
        local_kernel,
        out_shape=jax.ShapeDtypeStruct((2, CHUNK, 2, 2, 2, 2, ROWS, G), f32),
        grid_spec=pltpu.PrefetchScalarGridSpec(
            num_scalar_prefetch=1,
            grid=(2, 2, 2),
            in_specs=[pl.BlockSpec((None, 2, None, 2, 2, CHUNK, 8, G), lambda i, j, r, g: (i, 0, j, 0, 0, 0, r, 0))],
            out_specs=pl.BlockSpec((2, CHUNK, None, 2, None, 2, 8, G), lambda i, j, r, g: (0, 0, i, 0, j, 0, r, 0)),
            scratch_shapes=[pltpu.VMEM((2, 2, 2, CHUNK, 8, G), f32)],
        ),
        cost_estimate=cost(1),
        compiler_params=params(16),
        name="local",
    )(gates, x.reshape(2, 2, 2, 2, 2, CHUNK, ROWS, G)).reshape(2, CHUNK, G, G)


def narrow_kernel(bit_ref, gate_ref, own_ref, far_ref, *refs):
    out_ref = refs[-1]
    coef = narrow_coef(gate_ref, bit_ref[0])

    def tile(step, carry):
        rows = pl.ds(pl.multiple_of(step * 8, 8), 8)
        for h1 in range(2):
            amps = [
                tuple(ref[c, 2 * h1 + h0, rows, :] for c in range(2)) for ref in (own_ref, far_ref) for h0 in range(2)
            ]
            for h0, (real, imag) in enumerate(combine(coef, amps, 2)):
                out_ref[0, 2 * h1 + h0, rows, :] = real
                out_ref[1, 2 * h1 + h0, rows, :] = imag
        return carry

    lax.fori_loop(0, 8, tile, 0)


def narrow(bit, gates, own, far, group, held, weight=1):
    source = pl.BlockSpec((2, CHUNK, 64, G), lambda i, s, g: (0, 0, i, 0))
    extra = [] if held is None else [held.reshape(2, 4, CHUNK, G, G)]
    return pl.pallas_call(
        narrow_kernel,
        out_shape=jax.ShapeDtypeStruct((2, 4, CHUNK, G, G), f32),
        grid_spec=pltpu.PrefetchScalarGridSpec(
            num_scalar_prefetch=2,
            grid=(4,),
            in_specs=[source, source] + [pl.BlockSpec(memory_space=pl.ANY)] * len(extra),
            out_specs=pl.BlockSpec((2, None, CHUNK, 64, G), lambda i, s, g: (0, group, 0, i, 0)),
        ),
        input_output_aliases={4: 0} if extra else {},
        cost_estimate=cost(weight),
        compiler_params=params(16),
        name="narrow",
    )(bit, gates, own, far, *extra)


def pair_kernel(bit_ref, gate_ref, own_ref, far_ref, held_ref, out_ref, back_ref, scratch):
    for n, ref in enumerate((own_ref, far_ref)):
        wide_high(gate_ref, ref, scratch.at[n])
    coef = narrow_coef(gate_ref, bit_ref[0])
    for w2 in range(2):
        for h1 in range(2):
            state = [wide_low(gate_ref, scratch.at[n], w2, h1) for n in range(2)]
            for w0 in range(2):
                where = [(n, h0) for n in range(2) for h0 in range(2)]
                values = combine(coef, [state[n][w0, h0] for n, h0 in where])
                for (n, h0), (real, imag) in zip(where, values):
                    target = (out_ref, back_ref)[n]
                    target[0, 2 * h1 + h0, w2, w0] = real
                    target[1, 2 * h1 + h0, w2, w0] = imag


def pair(bit, gates, both, half, held):
    def source(part):
        return pl.BlockSpec(
            (None, 2, None, 2, 2, None, CHUNK, 8, G), lambda i, j, s, g: (i, 0, j, 0, 0, part, 0, 0, 0)
        )

    both = both.reshape(2, 2, 2, 2, 2, 2, CHUNK, 8, G)
    full = (2, 4, CHUNK, 2, 2, 2, 2, ROWS, G)
    back = (2, CHUNK, 2, 2, 2, 2, 8, G)
    held, back = pl.pallas_call(
        pair_kernel,
        out_shape=[jax.ShapeDtypeStruct(full, f32), jax.ShapeDtypeStruct(back, f32)],
        grid_spec=pltpu.PrefetchScalarGridSpec(
            num_scalar_prefetch=2,
            grid=(2, 2),
            in_specs=[source(0), source(1), pl.BlockSpec(memory_space=pl.ANY)],
            out_specs=[
                pl.BlockSpec(
                    (2, None, CHUNK, None, 2, None, 2, 8, G),
                    lambda i, j, s, g: (0, 2 * s[0], 0, i, 0, j, 0, half, 0),
                ),
                pl.BlockSpec((2, CHUNK, None, 2, None, 2, 8, G), lambda i, j, s, g: (0, 0, i, 0, j, 0, 0, 0)),
            ],
            scratch_shapes=[pltpu.VMEM((2, 2, 2, 2, CHUNK, 8, G), f32)],
        ),
        input_output_aliases={4: 0},
        cost_estimate=cost(1),
        compiler_params=params(16),
        name="pair",
    )(bit, gates, both, both, held.reshape(full))
    return held, back.reshape(2, CHUNK, G // ROWS, 8, G)


def place_kernel(bit_ref, piece_ref, held_ref, out_ref):
    out_ref[...] = piece_ref[...]


def place(bit, piece, half, held, weight=1):
    full = (2, 4, CHUNK, G // ROWS, ROWS, G)
    return pl.pallas_call(
        place_kernel,
        out_shape=jax.ShapeDtypeStruct(full, f32),
        grid_spec=pltpu.PrefetchScalarGridSpec(
            num_scalar_prefetch=1,
            grid=(CHUNK,),
            in_specs=[
                pl.BlockSpec((2, 1, G // ROWS, 8, G), lambda h, s: (0, h, 0, 0, 0)),
                pl.BlockSpec(memory_space=pl.ANY),
            ],
            out_specs=pl.BlockSpec(
                (2, None, 1, G // ROWS, 8, G), lambda h, s: (0, 2 * (1 - s[0]), h, 0, half, 0)
            ),
        ),
        input_output_aliases={2: 0},
        cost_estimate=cost(weight),
        compiler_params=params(16),
        name="place",
    )(bit, piece, held.reshape(full))


def body(amplitudes, low_gate, mid_gate, pair_gates):
    x = amplitudes.reshape(2, 16, G, G)
    bit = lax.axis_index("narrow") >> 1 & 1
    bits = bit.reshape(1).astype(jnp.int32)
    partners = [(i, i ^ 2) for i in range(lax.axis_size("narrow"))]
    barrier = lax.optimization_barrier

    def swapped(value):
        return lax.ppermute(value, "narrow", partners)

    def remap(value):
        return lax.all_to_all(value, "wide", split_axis=0, concat_axis=0, tiled=True)

    def group(value):
        return jnp.full((1,), value, jnp.int32)

    sent = lax.dynamic_slice_in_dim(x, 8 * (1 - bit), CHUNK, 1)
    bits, low_gate, sent = barrier((bits, low_gate, sent))
    arrived = swapped(sent)
    gates = prepare(low_gate, mid_gate)
    flat = pair_gates.reshape(96)

    first = local(flat, remap(merged(x, group(1), gates)[0]))
    own = merged(x, 2 * bits, gates, 2, 0)
    gates, own = barrier((gates, own))
    second = merged(x, group(3), gates)[0]
    second, first = barrier((second, first))
    second = local(flat, remap(second))
    far = merged(arrived, group(0), gates, 2, 1, own, 30000000000)
    held = narrow(bits, flat, first, swapped(first), 1, None, 50000000000)
    backs = []
    for half in range(2):
        held, back = pair(bits, flat, remap(far[half]), half, held)
        backs.append(swapped(back))
    held = narrow(bits, flat, second, swapped(second), 3, held, 10000000000)
    for half in range(2):
        held = place(bits, backs[half], half, held, 1000000000)
    return held.reshape(amplitudes.shape)


def solution(mesh):
    in_specs = (P(None, "wide", "narrow", None, None, None), P(), P(), P())
    out_specs = P(None, "wide", "narrow", None, None, None)
    return jax.shard_map(body, mesh=mesh, in_specs=in_specs, out_specs=out_specs, check_vma=False)
```

```python
import jax
import jax.numpy as jnp
from jax import lax
from jax.experimental import pallas as pl
from jax.experimental.pallas import tpu as pltpu
from jax.sharding import PartitionSpec as P

f32, bf16 = jnp.float32, jnp.bfloat16
G = 256
ROWS = 16
CHUNK = 4
PAIR = 2
RETURNS = ((0, 0, 2), (1, 0, 1), (1, 1, 1))


def cost(weight):
    return pl.CostEstimate(flops=weight, bytes_accessed=1, transcendentals=0)


def params(mib):
    return pltpu.CompilerParams(vmem_limit_bytes=mib << 20)


def hbm(x):
    return pltpu.with_memory_space_constraint(x, pltpu.HBM)


def split(x):
    high = x.astype(bf16)
    return high, (x - high.astype(f32)).astype(bf16)


def prepare(low_ref, mid_ref, g_ref):
    for at, ref in enumerate((low_ref, mid_ref)):
        real, imag = ref[0], ref[1]
        for j, part in enumerate((real, imag - real, real + imag)):
            g_ref[at, j, 0], g_ref[at, j, 1] = split(part)


def merged_kernel(x_ref, g_ref, refs):

    def right(value, j):
        high, low = split(value)
        out = None
        for a, b in ((high, 0), (high, 1), (low, 0)):
            term = lax.dot_general(a, g_ref[0, j, b], (((1,), (1,)), ((), ())), preferred_element_type=f32)
            out = term if out is None else out + term
        return out

    def left(value, j):
        high, low = split(value)
        out = None
        for a, b in ((0, high), (0, low), (1, high)):
            term = jnp.dot(g_ref[1, j, a], b, preferred_element_type=f32)
            out = term if out is None else out + term
        return out

    def both(apply, real, imag):
        shared = apply(real + imag, 0)
        cross = apply(real, 1)
        return shared - apply(imag, 2), shared + cross

    firsts = [both(right, x_ref[0, i], x_ref[1, i]) for i in range(PAIR)]
    for i, first in enumerate(firsts):
        for c, value in enumerate(both(left, *first)):
            value = value.reshape(G // ROWS, ROWS, G)
            for at, o_ref in enumerate(refs):
                rows = ROWS // len(refs)
                o_ref[:, c, i] = value[:, at * rows : (at + 1) * rows]


def merged(x, start, gates, count=CHUNK, parts=1, part=0, held=(), weight=1):
    rows = ROWS // parts
    total = 2 * CHUNK if parts == 2 else count
    out = jax.ShapeDtypeStruct((G // ROWS, 2, total, rows, G), f32)
    spec = pl.BlockSpec((G // ROWS, 2, PAIR, rows, G), lambda i, s: (0, 0, part + i, 0, 0))
    gate = pl.BlockSpec((2, G, G), lambda i, s: (0, 0, 0))

    def kernel(start_ref, x_ref, low_ref, mid_ref, *refs):
        g_ref = refs[-1]

        @pl.when(pl.program_id(0) == 0)
        def _():
            prepare(low_ref, mid_ref, g_ref)

        merged_kernel(x_ref, g_ref, refs[len(held) : -1])

    return pl.pallas_call(
        kernel,
        out_shape=[out] * parts,
        grid_spec=pltpu.PrefetchScalarGridSpec(
            num_scalar_prefetch=1,
            grid=(count // PAIR,),
            in_specs=[pl.BlockSpec((2, PAIR, G, G), lambda i, s: (0, s[0] + i, 0, 0)), gate, gate]
            + [pl.BlockSpec(memory_space=pl.ANY)] * len(held),
            out_specs=[spec] * parts,
            scratch_shapes=[pltpu.VMEM((2, 3, 2, G, G), bf16)],
        ),
        input_output_aliases={4 + j: j for j in range(len(held))},
        cost_estimate=cost(weight),
        compiler_params=params(60),
        name="merged",
    )(start, hbm(x), *gates, *held)


def combine(coef, amps, rows=4):
    outs = []
    for row in range(rows):
        real = imag = None
        for col, (ar, ai) in enumerate(amps):
            cr, ci = coef(row, col)
            real = cr * ar - ci * ai if real is None else real + (cr * ar - ci * ai)
            imag = cr * ai + ci * ar if imag is None else imag + (cr * ai + ci * ar)
        outs.append((real, imag))
    return outs


def plain(gate_ref, k):
    def coef(row, col):
        return gate_ref[32 * k + 4 * row + col], gate_ref[32 * k + 16 + 4 * row + col]

    return coef


def narrow_coef(gate_ref, own):
    bit = (own, 1 - own)

    def coef(row, col):
        at = 64 + 4 * (2 * bit[row >> 1] + (row & 1)) + 2 * bit[col >> 1] + (col & 1)
        return gate_ref[at], gate_ref[at + 16]

    return coef


def wide_high(gate_ref, ref, out):
    for w0 in range(2):
        for h0 in range(2):
            where = [(w2, w0, 2 * h1 + h0) for w2 in range(2) for h1 in range(2)]
            amps = [(ref[a, b, 0, h], ref[a, b, 1, h]) for a, b, h in where]
            for (a, b, h), (real, imag) in zip(where, combine(plain(gate_ref, 1), amps)):
                out[a, b, 0, h], out[a, b, 1, h] = real, imag


def wide_low(gate_ref, ref, w2, h1):
    where = [(w0, h0) for w0 in range(2) for h0 in range(2)]
    amps = [(ref[w2, w0, 0, 2 * h1 + h0], ref[w2, w0, 1, 2 * h1 + h0]) for w0, h0 in where]
    return dict(zip(where, combine(plain(gate_ref, 0), amps)))


def local_kernel(gate_ref, x_ref, o_ref):
    for w1 in range(2):
        for w2 in range(2):
            for h1 in range(x_ref.shape[4] // 2):
                for (w0, h0), (real, imag) in wide_low(gate_ref, x_ref.at[:, w1], w2, h1).items():
                    o_ref[0, 2 * h1 + h0, w2, w1, w0] = real
                    o_ref[1, 2 * h1 + h0, w2, w1, w0] = imag


def local(gates, x):
    count = x.shape[2]
    return pl.pallas_call(
        local_kernel,
        out_shape=jax.ShapeDtypeStruct((2, count, 2, 2, 2, 2, ROWS, G), f32),
        grid_spec=pltpu.PrefetchScalarGridSpec(
            num_scalar_prefetch=1,
            grid=(2,),
            in_specs=[pl.BlockSpec((None, 2, 2, 2, 2, count, ROWS, G), lambda i, g: (i, 0, 0, 0, 0, 0, 0, 0))],
            out_specs=pl.BlockSpec((2, count, None, 2, 2, 2, ROWS, G), lambda i, g: (0, 0, i, 0, 0, 0, 0, 0)),
        ),
        cost_estimate=cost(1),
        compiler_params=params(16),
        name="local",
    )(gates, x.reshape(2, 2, 2, 2, 2, count, ROWS, G)).reshape(2, count, G, G)


def narrow_kernel(gate_ref, own, sources, out_ref, scratch):
    coef = narrow_coef(gate_ref, own)
    per = len(sources[0])
    for w2 in range(2):
        for w0 in range(2):
            for h1 in range(2):
                amps = []
                for refs in sources:
                    ref = refs[h1 * per // 2]
                    for h0 in range(2):
                        h = h0 if per == 2 else 2 * h1 + h0
                        amps.append((ref[0, h, w2, w0], ref[1, h, w2, w0]))
                for h0, (real, imag) in enumerate(combine(coef, amps, 2)):
                    scratch[w2, w0, 0, 2 * h1 + h0] = real
                    scratch[w2, w0, 1, 2 * h1 + h0] = imag
    for w0 in range(2):
        for h0 in range(2):
            where = [(w2, w0, 2 * h1 + h0) for w2 in range(2) for h1 in range(2)]
            amps = [(scratch[a, b, 0, h], scratch[a, b, 1, h]) for a, b, h in where]
            for (a, b, h), (real, imag) in zip(where, combine(plain(gate_ref, 1), amps)):
                out_ref[0, h, a, b], out_ref[1, h, a, b] = real, imag


def narrow(bit, gates, own, far, group, held, weight=1):
    per = len(own)
    count = CHUNK // per
    source = pl.BlockSpec((2, count, None, 2, None, 2, ROWS, G), lambda i, j, s, g: (0, 0, i, 0, j, 0, 0, 0))
    full = (2, 4, CHUNK, 2, 2, 2, 2, ROWS, G)
    extra = [] if held is None else [held.reshape(full)]

    def kernel(bit_ref, gate_ref, *refs):
        narrow_kernel(gate_ref, bit_ref[0], (refs[:per], refs[per : 2 * per]), refs[-2], refs[-1])

    return pl.pallas_call(
        kernel,
        out_shape=jax.ShapeDtypeStruct(full, f32),
        grid_spec=pltpu.PrefetchScalarGridSpec(
            num_scalar_prefetch=2,
            grid=(2, 2),
            in_specs=[source] * (2 * per) + [pl.BlockSpec(memory_space=pl.ANY)] * len(extra),
            out_specs=pl.BlockSpec(
                (2, None, CHUNK, None, 2, None, 2, ROWS, G), lambda i, j, s, g: (0, group, 0, i, 0, j, 0, 0, 0)
            ),
            scratch_shapes=[pltpu.VMEM((2, 2, 2, CHUNK, ROWS, G), f32)],
        ),
        input_output_aliases={2 + 2 * per: 0} if extra else {},
        cost_estimate=cost(weight),
        compiler_params=params(16),
        name="narrow",
    )(bit, gates, *(value.reshape(2, count, 2, 2, 2, 2, ROWS, G) for value in (*own, *far)), *extra)


def pair_kernel(bit_ref, gate_ref, own_ref, far_ref, held_ref, out_ref, back_ref, scratch):
    for n, ref in enumerate((own_ref, far_ref)):
        wide_high(gate_ref, ref, scratch.at[n])
    coef = narrow_coef(gate_ref, bit_ref[0])
    for w2 in range(2):
        for h1 in range(2):
            state = [wide_low(gate_ref, scratch.at[n], w2, h1) for n in range(2)]
            for w0 in range(2):
                where = [(n, h0) for n in range(2) for h0 in range(2)]
                values = combine(coef, [state[n][w0, h0] for n, h0 in where])
                for (n, h0), (real, imag) in zip(where, values):
                    target = (out_ref, back_ref)[n]
                    target[0, 2 * h1 + h0, w2, w0] = real
                    target[1, 2 * h1 + h0, w2, w0] = imag


def pair(bit, gates, both, half, first, count, held):
    def source(part):
        return pl.BlockSpec(
            (None, 2, None, 2, 2, None, CHUNK, 8, G), lambda i, j, s, g: (first + i, 0, j, 0, 0, part, 0, 0, 0)
        )

    both = both.reshape(2, 2, 2, 2, 2, 2, CHUNK, 8, G)
    full = (2, 4, CHUNK, 2, 2, 2, 2, ROWS, G)
    back = (2, CHUNK, count, 2, 2, 2, 8, G)
    held, back = pl.pallas_call(
        pair_kernel,
        out_shape=[jax.ShapeDtypeStruct(full, f32), jax.ShapeDtypeStruct(back, f32)],
        grid_spec=pltpu.PrefetchScalarGridSpec(
            num_scalar_prefetch=2,
            grid=(count, 2),
            in_specs=[source(0), source(1), pl.BlockSpec(memory_space=pl.ANY)],
            out_specs=[
                pl.BlockSpec(
                    (2, None, CHUNK, None, 2, None, 2, 8, G),
                    lambda i, j, s, g: (0, 2 * s[0], 0, first + i, 0, j, 0, half, 0),
                ),
                pl.BlockSpec((2, CHUNK, None, 2, None, 2, 8, G), lambda i, j, s, g: (0, 0, i, 0, j, 0, 0, 0)),
            ],
            scratch_shapes=[pltpu.VMEM((2, 2, 2, 2, CHUNK, 8, G), f32)],
        ),
        input_output_aliases={4: 0},
        cost_estimate=cost(1),
        compiler_params=params(16),
        name="pair",
    )(bit, gates, both, both, held.reshape(full))
    return held, back.reshape(2, CHUNK, 8 * count, 8, G)


def place_kernel(bit_ref, piece_ref, held_ref, out_ref):
    out_ref[...] = piece_ref[...]


def place(bit, piece, half, first, held, weight=1):
    full = (2, 4, CHUNK, G // ROWS, ROWS, G)
    wide = piece.shape[2]
    return pl.pallas_call(
        place_kernel,
        out_shape=jax.ShapeDtypeStruct(full, f32),
        grid_spec=pltpu.PrefetchScalarGridSpec(
            num_scalar_prefetch=1,
            grid=(CHUNK // 2,),
            in_specs=[
                pl.BlockSpec((2, 2, wide, 8, G), lambda h, s: (0, h, 0, 0, 0)),
                pl.BlockSpec(memory_space=pl.ANY),
            ],
            out_specs=pl.BlockSpec(
                (2, None, 2, wide, 8, G), lambda h, s: (0, 2 * (1 - s[0]), h, first, half, 0)
            ),
        ),
        input_output_aliases={2: 0},
        cost_estimate=cost(weight),
        compiler_params=params(16),
        name="place",
    )(bit, piece, held.reshape(full))


def body(amplitudes, low_gate, mid_gate, pair_gates):
    x = amplitudes.reshape(2, 16, G, G)
    bit = lax.axis_index("narrow") >> 1 & 1
    bits = bit.reshape(1).astype(jnp.int32)
    partners = [(i, i ^ 2) for i in range(lax.axis_size("narrow"))]
    barrier = lax.optimization_barrier

    def swapped(value):
        return lax.ppermute(value, "narrow", partners)

    def remap(value):
        return lax.all_to_all(value, "wide", split_axis=0, concat_axis=0, tiled=True)

    def group(value):
        return jnp.full((1,), value, jnp.int32)


    def piece(bit, part):
        return lax.dynamic_slice_in_dim(x, 8 * (1 - bit) + PAIR * part, PAIR, 1)

    flat = pair_gates.reshape(96)
    bits, low_gate, sent = barrier((bits, low_gate, piece(bit, 0)))
    arrived = [swapped(sent)]
    gates = (low_gate, mid_gate)
    early = merged(x, group(2), gates, PAIR)[0]
    later, low_gate, early = barrier((bits, low_gate, early))
    arrived.append(swapped(piece(later[0], 1)))
    gates = (low_gate, mid_gate)
    late = merged(x, group(3), gates, PAIR)[0]
    own = merged(x, 4 * later, gates, CHUNK, 2, 0)
    first = [local(flat, remap(early))]
    own, late, low_gate, first[0] = barrier((own, late, low_gate, first[0]))
    second = merged(x, group(6), (low_gate, mid_gate))[0]
    first.append(local(flat, remap(late)))
    second = local(flat, remap(second))
    both = own
    distant = [swapped(value) for value in first]
    arrived[1], distant[0] = barrier((arrived[1], distant[0]))
    for part in range(2):
        both = merged(arrived[part], group(0), gates, PAIR, 2, 2 + part, both, (30000000000, 30000000000)[part])
    held = narrow(bits, flat, first, distant, 1, None, 20000000000)
    both = list(both)
    both[1], held = barrier((both[1], held))
    both[0], second = barrier((both[0], second))
    front, rest = remap(both[0]), remap(both[1])
    backs = []
    for half, first_wide, count in RETURNS:
        held, back = pair(bits, flat, (front, rest)[half], half, first_wide, count, held)
        backs.append(swapped(back))
        if half == 0:
            held = narrow(bits, flat, [second], [swapped(second)], 3, held, 25000000000)
    for back, (half, first_wide, _) in zip(backs, RETURNS):
        held = place(bits, back, half, first_wide, held, 1000000000)
    return held.reshape(amplitudes.shape)


def solution(mesh):
    in_specs = (P(None, "wide", "narrow", None, None, None), P(), P(), P())
    out_specs = P(None, "wide", "narrow", None, None, None)
    return jax.shard_map(body, mesh=mesh, in_specs=in_specs, out_specs=out_specs, check_vma=False)
```

```python
import jax
import jax.numpy as jnp
from jax import lax
from jax.experimental import pallas as pl
from jax.experimental.pallas import tpu as pltpu
from jax.sharding import PartitionSpec as P

f32, bf16 = jnp.float32, jnp.bfloat16
G = 256
ROWS = 16
CHUNK = 4
PAIR = 2
RETURNS = ((0, 0, 2), (1, 0, 1), (1, 1, 1))


def cost(weight):
    return pl.CostEstimate(flops=weight, bytes_accessed=1, transcendentals=0)


def params(mib):
    return pltpu.CompilerParams(vmem_limit_bytes=mib << 20)


def hbm(x):
    return pltpu.with_memory_space_constraint(x, pltpu.HBM)


def split(x):
    high = x.astype(bf16)
    return high, (x - high.astype(f32)).astype(bf16)


def prepare(low_ref, mid_ref, g_ref):
    for at, ref in enumerate((low_ref, mid_ref)):
        real, imag = ref[0], ref[1]
        for j, part in enumerate((real, imag - real, real + imag)):
            g_ref[at, j, 0], g_ref[at, j, 1] = split(part)


def merged_kernel(x_ref, g_ref, refs):

    def right(value, j):
        high, low = split(value)
        out = None
        for a, b in ((high, 0), (high, 1), (low, 0)):
            term = lax.dot_general(a, g_ref[0, j, b], (((1,), (1,)), ((), ())), preferred_element_type=f32)
            out = term if out is None else out + term
        return out

    def left(value, j):
        high, low = split(value)
        out = None
        for a, b in ((0, high), (0, low), (1, high)):
            term = jnp.dot(g_ref[1, j, a], b, preferred_element_type=f32)
            out = term if out is None else out + term
        return out

    def both(apply, real, imag):
        shared = apply(real + imag, 0)
        cross = apply(real, 1)
        return shared - apply(imag, 2), shared + cross

    firsts = [both(right, x_ref[0, i], x_ref[1, i]) for i in range(PAIR)]
    for i, first in enumerate(firsts):
        for c, value in enumerate(both(left, *first)):
            value = value.reshape(G // ROWS, ROWS, G)
            for at, o_ref in enumerate(refs):
                rows = ROWS // len(refs)
                o_ref[:, c, i] = value[:, at * rows : (at + 1) * rows]


def merged(x, start, gates, count=CHUNK, parts=1, part=0, held=(), weight=1):
    rows = ROWS // parts
    total = 2 * CHUNK if parts == 2 else count
    out = jax.ShapeDtypeStruct((G // ROWS, 2, total, rows, G), f32)
    spec = pl.BlockSpec((G // ROWS, 2, PAIR, rows, G), lambda i, s: (0, 0, part + i, 0, 0))
    gate = pl.BlockSpec((2, G, G), lambda i, s: (0, 0, 0))

    def kernel(start_ref, x_ref, low_ref, mid_ref, *refs):
        g_ref = refs[-1]

        @pl.when(pl.program_id(0) == 0)
        def _():
            prepare(low_ref, mid_ref, g_ref)

        merged_kernel(x_ref, g_ref, refs[len(held) : -1])

    return pl.pallas_call(
        kernel,
        out_shape=[out] * parts,
        grid_spec=pltpu.PrefetchScalarGridSpec(
            num_scalar_prefetch=1,
            grid=(count // PAIR,),
            in_specs=[pl.BlockSpec((2, PAIR, G, G), lambda i, s: (0, s[0] + i, 0, 0)), gate, gate]
            + [pl.BlockSpec(memory_space=pl.ANY)] * len(held),
            out_specs=[spec] * parts,
            scratch_shapes=[pltpu.VMEM((2, 3, 2, G, G), bf16)],
        ),
        input_output_aliases={4 + j: j for j in range(len(held))},
        cost_estimate=cost(weight),
        compiler_params=params(60),
        name="merged",
    )(start, hbm(x), *gates, *held)


def combine(coef, amps, rows=4):
    outs = []
    for row in range(rows):
        real = imag = None
        for col, (ar, ai) in enumerate(amps):
            cr, ci = coef(row, col)
            real = cr * ar - ci * ai if real is None else real + (cr * ar - ci * ai)
            imag = cr * ai + ci * ar if imag is None else imag + (cr * ai + ci * ar)
        outs.append((real, imag))
    return outs


def plain(gate_ref, k):
    def coef(row, col):
        return gate_ref[32 * k + 4 * row + col], gate_ref[32 * k + 16 + 4 * row + col]

    return coef


def narrow_coef(gate_ref, own):
    bit = (own, 1 - own)

    def coef(row, col):
        at = 64 + 4 * (2 * bit[row >> 1] + (row & 1)) + 2 * bit[col >> 1] + (col & 1)
        return gate_ref[at], gate_ref[at + 16]

    return coef


def wide_high(gate_ref, ref, out):
    for w0 in range(2):
        for h0 in range(2):
            where = [(w2, w0, 2 * h1 + h0) for w2 in range(2) for h1 in range(2)]
            amps = [(ref[a, b, 0, h], ref[a, b, 1, h]) for a, b, h in where]
            for (a, b, h), (real, imag) in zip(where, combine(plain(gate_ref, 1), amps)):
                out[a, b, 0, h], out[a, b, 1, h] = real, imag


def wide_low(gate_ref, ref, w2, h1):
    where = [(w0, h0) for w0 in range(2) for h0 in range(2)]
    amps = [(ref[w2, w0, 0, 2 * h1 + h0], ref[w2, w0, 1, 2 * h1 + h0]) for w0, h0 in where]
    return dict(zip(where, combine(plain(gate_ref, 0), amps)))


def local_kernel(gate_ref, x_ref, o_ref):
    for w1 in range(2):
        for w2 in range(2):
            for h1 in range(x_ref.shape[4] // 2):
                for (w0, h0), (real, imag) in wide_low(gate_ref, x_ref.at[:, w1], w2, h1).items():
                    o_ref[0, 2 * h1 + h0, w2, w1, w0] = real
                    o_ref[1, 2 * h1 + h0, w2, w1, w0] = imag


def local(gates, x):
    count = x.shape[2]
    return pl.pallas_call(
        local_kernel,
        out_shape=jax.ShapeDtypeStruct((2, count, 2, 2, 2, 2, ROWS, G), f32),
        grid_spec=pltpu.PrefetchScalarGridSpec(
            num_scalar_prefetch=1,
            grid=(2,),
            in_specs=[pl.BlockSpec((None, 2, 2, 2, 2, count, ROWS, G), lambda i, g: (i, 0, 0, 0, 0, 0, 0, 0))],
            out_specs=pl.BlockSpec((2, count, None, 2, 2, 2, ROWS, G), lambda i, g: (0, 0, i, 0, 0, 0, 0, 0)),
        ),
        cost_estimate=cost(1),
        compiler_params=params(16),
        name="local",
    )(gates, x.reshape(2, 2, 2, 2, 2, count, ROWS, G)).reshape(2, count, G, G)


def narrow_kernel(gate_ref, own, sources, out_ref, scratch):
    coef = narrow_coef(gate_ref, own)
    per = len(sources[0])
    for w2 in range(2):
        for w0 in range(2):
            for h1 in range(2):
                amps = []
                for refs in sources:
                    ref = refs[h1 * per // 2]
                    for h0 in range(2):
                        h = h0 if per == 2 else 2 * h1 + h0
                        amps.append((ref[0, h, w2, w0], ref[1, h, w2, w0]))
                for h0, (real, imag) in enumerate(combine(coef, amps, 2)):
                    scratch[w2, w0, 0, 2 * h1 + h0] = real
                    scratch[w2, w0, 1, 2 * h1 + h0] = imag
    for w0 in range(2):
        for h0 in range(2):
            where = [(w2, w0, 2 * h1 + h0) for w2 in range(2) for h1 in range(2)]
            amps = [(scratch[a, b, 0, h], scratch[a, b, 1, h]) for a, b, h in where]
            for (a, b, h), (real, imag) in zip(where, combine(plain(gate_ref, 1), amps)):
                out_ref[0, h, a, b], out_ref[1, h, a, b] = real, imag


def narrow(bit, gates, own, far, group, held, weight=1):
    per = len(own)
    count = CHUNK // per
    source = pl.BlockSpec((2, count, None, 2, None, 2, ROWS, G), lambda i, j, s, g: (0, 0, i, 0, j, 0, 0, 0))
    full = (2, 4, CHUNK, 2, 2, 2, 2, ROWS, G)
    extra = [] if held is None else [held.reshape(full)]

    def kernel(bit_ref, gate_ref, *refs):
        narrow_kernel(gate_ref, bit_ref[0], (refs[:per], refs[per : 2 * per]), refs[-2], refs[-1])

    return pl.pallas_call(
        kernel,
        out_shape=jax.ShapeDtypeStruct(full, f32),
        grid_spec=pltpu.PrefetchScalarGridSpec(
            num_scalar_prefetch=2,
            grid=(2, 2),
            in_specs=[source] * (2 * per) + [pl.BlockSpec(memory_space=pl.ANY)] * len(extra),
            out_specs=pl.BlockSpec(
                (2, None, CHUNK, None, 2, None, 2, ROWS, G), lambda i, j, s, g: (0, group, 0, i, 0, j, 0, 0, 0)
            ),
            scratch_shapes=[pltpu.VMEM((2, 2, 2, CHUNK, ROWS, G), f32)],
        ),
        input_output_aliases={2 + 2 * per: 0} if extra else {},
        cost_estimate=cost(weight),
        compiler_params=params(16),
        name="narrow",
    )(bit, gates, *(value.reshape(2, count, 2, 2, 2, 2, ROWS, G) for value in (*own, *far)), *extra)


def pair_kernel(bit_ref, gate_ref, own_ref, far_ref, held_ref, out_ref, back_ref, scratch):
    for n, ref in enumerate((own_ref, far_ref)):
        wide_high(gate_ref, ref, scratch.at[n])
    coef = narrow_coef(gate_ref, bit_ref[0])
    for w2 in range(2):
        for h1 in range(2):
            state = [wide_low(gate_ref, scratch.at[n], w2, h1) for n in range(2)]
            for w0 in range(2):
                where = [(n, h0) for n in range(2) for h0 in range(2)]
                values = combine(coef, [state[n][w0, h0] for n, h0 in where])
                for (n, h0), (real, imag) in zip(where, values):
                    target = (out_ref, back_ref)[n]
                    target[0, 2 * h1 + h0, w2, w0] = real
                    target[1, 2 * h1 + h0, w2, w0] = imag


def pair(bit, gates, both, half, first, count, held):
    def source(part):
        return pl.BlockSpec(
            (None, 2, None, 2, 2, None, CHUNK, 8, G), lambda i, j, s, g: (first + i, 0, j, 0, 0, part, 0, 0, 0)
        )

    both = both.reshape(2, 2, 2, 2, 2, 2, CHUNK, 8, G)
    full = (2, 4, CHUNK, 2, 2, 2, 2, ROWS, G)
    back = (2, CHUNK, count, 2, 2, 2, 8, G)
    held, back = pl.pallas_call(
        pair_kernel,
        out_shape=[jax.ShapeDtypeStruct(full, f32), jax.ShapeDtypeStruct(back, f32)],
        grid_spec=pltpu.PrefetchScalarGridSpec(
            num_scalar_prefetch=2,
            grid=(count, 2),
            in_specs=[source(0), source(1), pl.BlockSpec(memory_space=pl.ANY)],
            out_specs=[
                pl.BlockSpec(
                    (2, None, CHUNK, None, 2, None, 2, 8, G),
                    lambda i, j, s, g: (0, 2 * s[0], 0, first + i, 0, j, 0, half, 0),
                ),
                pl.BlockSpec((2, CHUNK, None, 2, None, 2, 8, G), lambda i, j, s, g: (0, 0, i, 0, j, 0, 0, 0)),
            ],
            scratch_shapes=[pltpu.VMEM((2, 2, 2, 2, CHUNK, 8, G), f32)],
        ),
        input_output_aliases={4: 0},
        cost_estimate=cost(1),
        compiler_params=params(16),
        name="pair",
    )(bit, gates, hbm(both), hbm(both), held.reshape(full))
    return held, back.reshape(2, CHUNK, 8 * count, 8, G)


def place_kernel(bit_ref, piece_ref, held_ref, out_ref):
    out_ref[...] = piece_ref[...]


def place(bit, piece, half, first, held, weight=1):
    full = (2, 4, CHUNK, G // ROWS, ROWS, G)
    wide = piece.shape[2]
    return pl.pallas_call(
        place_kernel,
        out_shape=jax.ShapeDtypeStruct(full, f32),
        grid_spec=pltpu.PrefetchScalarGridSpec(
            num_scalar_prefetch=1,
            grid=(1,),
            in_specs=[
                pl.BlockSpec((2, CHUNK, wide, 8, G), lambda h, s: (0, h, 0, 0, 0)),
                pl.BlockSpec(memory_space=pl.ANY),
            ],
            out_specs=pl.BlockSpec(
                (2, None, CHUNK, wide, 8, G), lambda h, s: (0, 2 * (1 - s[0]), h, first, half, 0)
            ),
        ),
        input_output_aliases={2: 0},
        cost_estimate=cost(weight),
        compiler_params=params(16),
        name="place",
    )(bit, piece, held.reshape(full))


def body(amplitudes, low_gate, mid_gate, pair_gates):
    x = amplitudes.reshape(2, 16, G, G)
    bit = lax.axis_index("narrow") >> 1 & 1
    bits = bit.reshape(1).astype(jnp.int32)
    partners = [(i, i ^ 2) for i in range(lax.axis_size("narrow"))]
    barrier = lax.optimization_barrier

    def swapped(value):
        return lax.ppermute(value, "narrow", partners)

    def remap(value):
        return lax.all_to_all(value, "wide", split_axis=0, concat_axis=0, tiled=True)

    def group(value):
        return jnp.full((1,), value, jnp.int32)


    def piece(bit, part):
        return lax.dynamic_slice_in_dim(x, 8 * (1 - bit) + PAIR * part, PAIR, 1)

    flat = pair_gates.reshape(96)
    bits, low_gate, sent = barrier((bits, low_gate, piece(bit, 0)))
    arrived = [swapped(sent)]
    gates = (low_gate, mid_gate)
    early = merged(x, group(2), gates, PAIR)[0]
    later, low_gate, early = barrier((bits, low_gate, early))
    arrived.append(swapped(piece(later[0], 1)))
    gates = (low_gate, mid_gate)
    late = merged(x, group(3), gates, PAIR)[0]
    own = merged(x, 4 * later, gates, CHUNK, 2, 0)
    first = [local(flat, remap(early))]
    own, late, low_gate, first[0] = barrier((own, late, low_gate, first[0]))
    second = merged(x, group(6), (low_gate, mid_gate))[0]
    first.append(local(flat, remap(late)))
    second = local(flat, remap(second))
    both = own
    distant = [swapped(value) for value in first]
    arrived[1], distant[0] = barrier((arrived[1], distant[0]))
    for part in range(2):
        both = merged(arrived[part], group(0), gates, PAIR, 2, 2 + part, both, (30000000000, 30000000000)[part])
    held = narrow(bits, flat, first, distant, 1, None, 20000000000)
    both = list(both)
    both[1], held = barrier((both[1], held))
    both[0], second = barrier((both[0], second))
    front, rest = remap(both[0]), remap(both[1])
    backs = []
    for half, first_wide, count in RETURNS:
        held, back = pair(bits, flat, (front, rest)[half], half, first_wide, count, held)
        backs.append(swapped(back))
        if half == 0:
            held = narrow(bits, flat, [second], [swapped(second)], 3, held, 25000000000)
    for back, (half, first_wide, _) in zip(backs, RETURNS):
        held = place(bits, back, half, first_wide, held, 1000000000)
    return held.reshape(amplitudes.shape)


def solution(mesh):
    in_specs = (P(None, "wide", "narrow", None, None, None), P(), P(), P())
    out_specs = P(None, "wide", "narrow", None, None, None)
    return jax.shard_map(body, mesh=mesh, in_specs=in_specs, out_specs=out_specs, check_vma=False)
```
